32 devices in a mesh: rows: 4 (over y, x), grid: 8 (over z, core).
Axes of the slice: x: 2, y: 2, z: 4, core: 2. Of those that a mesh axis runs over, the one named last changes fastest.
Arguments:
- positions: int32 [2, 2048], P(None, 'rows'), may hold values from 0 to 63, as said below
- angles: int32 [2, 4096], P(None, 'grid'), may hold values from 0 to 4095
- subspace: bfloat16 [2, 2048, 1920], P(None, 'rows', 'grid')
Outputs:
- spectrum: float32 [4096], P('grid')
The draws below stay inside these ranges and needn't reach their ends.
Inputs may be any that keep to these rules, and one draw needn't show every extreme that they name: `positions`: each column names a distinct lattice point; both coordinates lie in 0 to 63.
All inputs are finite; a program needn't handle non-finite values.
Results may differ from the reference program's by a relative error of at most 0.0012.
Values may be sent and summed in bfloat16 or wider, within the bound.
A program may use at most 64 MiB of HBM per device.

```python
import math
import jax
import jax.numpy as jnp
from jax import lax

ELEMENTS = 2048
NOISE = 1920
SOURCES = 128
LATTICE = 64
PHASES = 4096
ANG_DEV = 512
ANGLES = 4096


def lattice_points(key):
    chosen = jax.random.permutation(jax.random.fold_in(key, 11), LATTICE * LATTICE)[:ELEMENTS]
    return jnp.stack([chosen // LATTICE, chosen % LATTICE]).astype(jnp.int32)


def grid_points(key):
    return jax.random.randint(jax.random.fold_in(key, 12), (2, ANGLES), 0, PHASES, dtype=jnp.int32)


def draw_positions(key, part):
    return lattice_points(key)


def draw_angles(key, part):
    return grid_points(key)


def draw_subspace(key, part):
    placed = lattice_points(key)
    grid_all = grid_points(key)
    chosen = jax.random.permutation(jax.random.fold_in(key, 13), ANGLES)[:SOURCES]
    source_angles = grid_all[:, chosen]
    phase_index = (placed[0][:, None] * source_angles[0][None, :] + placed[1][:, None] * source_angles[1][None, :]) % PHASES
    phase = phase_index.astype(jnp.float32) * (2.0 * math.pi / PHASES)
    source_re = jnp.cos(phase)
    source_im = jnp.sin(phase)
    spread = (2.0 * ELEMENTS) ** (-0.5)
    noise_re = spread * jax.random.normal(jax.random.fold_in(key, 14), (ELEMENTS, NOISE), jnp.float32)
    noise_im = spread * jax.random.normal(jax.random.fold_in(key, 15), (ELEMENTS, NOISE), jnp.float32)
    high = lax.Precision.HIGHEST
    coeff_re = (jnp.dot(source_re.T, noise_re, precision=high) + jnp.dot(source_im.T, noise_im, precision=high)) / ELEMENTS
    coeff_im = (jnp.dot(source_re.T, noise_im, precision=high) - jnp.dot(source_im.T, noise_re, precision=high)) / ELEMENTS
    result_re = noise_re - (jnp.dot(source_re, coeff_re, precision=high) - jnp.dot(source_im, coeff_im, precision=high))
    result_im = noise_im - (jnp.dot(source_re, coeff_im, precision=high) + jnp.dot(source_im, coeff_re, precision=high))
    return jnp.stack([result_re, result_im]).astype(jnp.bfloat16)


def setup_inputs(seed: int = 0) -> dict:
    splits = jax.random.split(jax.random.key(seed), 4)
    positions = draw_positions(jax.random.fold_in(splits[3], 71), 0)
    angles = draw_angles(jax.random.fold_in(splits[3], 71), 0)
    subspace = draw_subspace(jax.random.fold_in(splits[3], 71), 0)
    return dict(positions=positions, angles=angles, subspace=subspace)


def steering_block(positions, angle_block):
    phase_index = (positions[0][:, None] * angle_block[0][None, :] + positions[1][:, None] * angle_block[1][None, :]) % PHASES
    phase = phase_index.astype(jnp.float32) * (2.0 * math.pi / PHASES)
    return jnp.concatenate([jnp.cos(phase), jnp.sin(phase)], 0).astype(jnp.bfloat16)


def reference(positions, angles, subspace):
    real_part = subspace[0]
    imag_part = subspace[1]
    upper_half = jnp.concatenate([real_part, imag_part], 0)
    lower_half = jnp.concatenate([-imag_part, real_part], 0)
    stacked = jnp.stack([upper_half, lower_half]).astype(jnp.float32)
    blocks = ANGLES // ANG_DEV
    angle_blocks = jnp.transpose(angles.reshape(2, blocks, ANG_DEV), (1, 0, 2))

    def one_block(angle_block):
        steering = steering_block(positions, angle_block).astype(jnp.float32)
        projected = jnp.einsum("pmk,ma->pka", stacked, steering)
        squares = jnp.sum(projected * projected, axis=(0, 1))
        return 1.0 / (squares / NOISE + 1e-6)

    return lax.map(one_block, angle_blocks).reshape(ANGLES)
```

```python
import functools

import jax
import jax.numpy as jnp
from jax import lax
from jax.experimental import pallas as pl
from jax.experimental.pallas import tpu as pltpu
from jax.sharding import PartitionSpec as P

PHASES = 4096
LOADING = 1e-06
MESH = pl.DeviceIdType.MESH
LANES = 128
TILE = 256
CHUNK = 64

COS_ODD = (-6.283164024353027, 41.33714294433594, -81.34076690673828, 70.9933853149414)
SIN_EVEN = (
    0.9999999403953552,
    -19.739171981811523,
    64.9345932006836,
    -85.24032592773438,
    56.242347717285156,
)


def horner(coefficients, x):
    total = coefficients[-1] * x + coefficients[-2]
    for c in coefficients[-3::-1]:
        total = total * x + c
    return total


def cos_sin(turns):
    r = turns - jnp.round(turns)
    w = jnp.abs(r) - 0.25
    w2 = w * w
    cos = horner(COS_ODD, w2) * w
    sin = horner(SIN_EVEN, w2)
    return cos, jnp.where(r < 0.0, -sin, sin)


def flip(bit, by):
    return 1 - bit if by else bit


def kernel(
    rows, grid, noise, pos_ref, ang_ref, v_ref, out_ref,
    pos, ang, acol, v, lhs_a, lhs_b, acc, part, red,
    ang_send, ang_recv, pos_send, pos_recv, own_sem,
    row_send, row_recv, core_send, core_recv, red_send, red_recv,
):
    r, g = lax.axis_index("rows"), lax.axis_index("grid")
    half, y = r % 2, r // 2
    core, chip = g % 2, g // 2
    blocks = grid // 4
    group = y * 2 + core
    per_block = ang_ref.shape[1]
    elements = pos_ref.shape[1]
    tiles = blocks * per_block // TILE

    def row_partner(j):
        return flip(y, j // 2) * 2 + flip(half, j % 2)

    barrier = pltpu.get_barrier_semaphore()
    for j in range(1, 4):
        pl.semaphore_signal(barrier, inc=1, device_id=(row_partner(j), g), device_id_type=MESH)

    def greet(d, carry):
        pl.semaphore_signal(barrier, inc=1, device_id=(r, (g + d) % grid), device_id_type=MESH)
        return carry

    lax.fori_loop(1, grid, greet, 0)
    pl.semaphore_wait(barrier, 3 + grid - 1)

    pos_copies = []
    for j in range(1, 4):
        pos_copies.append(pltpu.make_async_remote_copy(
            pos_ref, pos.at[j], pos_send.at[j], pos_recv.at[j],
            device_id=(row_partner(j), g), device_id_type=MESH))
        pos_copies[-1].start()

    def send_angles(d, carry):
        pltpu.make_async_remote_copy(
            ang_ref, ang.at[g], ang_send, ang_recv,
            device_id=(r, (g + d) % grid), device_id_type=MESH).start()
        return carry

    lax.fori_loop(1, grid, send_angles, 0)
    pltpu.make_async_copy(ang_ref, ang.at[g], ang_recv).start()

    row_copies = []
    for j in range(1, 4):
        row_copies.append(pltpu.make_async_remote_copy(
            v_ref.at[flip(half, j % 2)], v.at[j, core], row_send.at[j], row_recv.at[j],
            device_id=(row_partner(j), g), device_id_type=MESH))

    def core_copy(j, source):
        return pltpu.make_async_remote_copy(
            source, v.at[j, core], core_send.at[j], core_recv.at[j],
            device_id=(r, chip * 2 + 1 - core), device_id_type=MESH)

    core_copies = [core_copy(0, v_ref.at[half])] + [core_copy(j, v.at[j, core]) for j in range(1, 4)]
    core_copies[0].start()
    own_copy = pltpu.make_async_copy(v_ref.at[half], v.at[0, core], own_sem)
    own_copy.start()
    for copy in row_copies:
        copy.start()

    pos[0] = pos_ref[...]
    pltpu.make_async_copy(ang, ang, ang_recv).wait()
    for i in range(blocks):
        for k in range(2):
            line = ang[group * blocks + i, k : k + 1, :].astype(jnp.float32) * (1.0 / PHASES)
            acol[k, i * per_block : (i + 1) * per_block, :] = jnp.broadcast_to(line, (LANES, per_block)).T
    for copy in pos_copies:
        copy.wait_recv()

    def steer(step, lhs):
        j, tile = step // tiles, step % tiles
        p = pos[j].astype(jnp.float32)
        start = pl.multiple_of(tile * TILE, TILE)
        for row in range(0, TILE, CHUNK):
            a0 = acol[0, pl.ds(start + row, CHUNK), :]
            a1 = acol[1, pl.ds(start + row, CHUNK), :]
            for lane in range(0, elements, LANES):
                turns = a0 * p[0:1, lane : lane + LANES] + a1 * p[1:2, lane : lane + LANES]
                cos, sin = cos_sin(turns)
                cos, sin = cos.astype(jnp.bfloat16), sin.astype(jnp.bfloat16)
                lhs[row : row + CHUNK, lane : lane + LANES] = cos
                lhs[row : row + CHUNK, elements + lane : elements + lane + LANES] = sin
                lhs[TILE + row : TILE + row + CHUNK, lane : lane + LANES] = sin
                lhs[TILE + row : TILE + row + CHUNK, elements + lane : elements + lane + LANES] = -cos

    width = v.shape[-1]

    def project(j, tile, lhs):
        columns = jnp.concatenate(
            [v[j, 0].reshape(2 * elements, width), v[j, 1].reshape(2 * elements, width)], 1)
        product = jnp.dot(lhs[...], columns, preferred_element_type=jnp.float32)
        if j == 0:
            acc[tile] = product
        else:
            acc[tile] += product

    last = 4 * tiles - 1

    def run(j):
        @pl.loop(0, tiles // 2)
        def _(pair):
            step = j * tiles + 2 * pair
            steer(step + 1, lhs_b)
            project(j, 2 * pair, lhs_a)
            steer(jnp.minimum(step + 2, last), lhs_a)
            project(j, 2 * pair + 1, lhs_b)

    steer(0, lhs_a)
    own_copy.wait()
    core_copies[0].wait_recv()
    run(0)
    for j in (1, 2):
        row_copies[j - 1].wait_recv()
        core_copies[j].start()
    core_copies[1].wait_recv()
    run(1)
    row_copies[2].wait_recv()
    core_copies[3].start()
    core_copies[2].wait_recv()
    run(2)
    core_copies[3].wait_recv()
    run(3)

    for tile in range(tiles):
        sums = acc[tile, 0:TILE] * acc[tile, 0:TILE] + acc[tile, TILE:] * acc[tile, TILE:]
        folded = sums[:, 0:LANES]
        for lane in range(LANES, sums.shape[1], LANES):
            folded = folded + sums[:, lane : lane + LANES]
        offset = tile * TILE % per_block
        part[tile * TILE // per_block, :, offset : offset + TILE] = jnp.sum(folded.T, axis=0, keepdims=True)

    slot = half * (grid // 2) + chip
    transfers = []
    for i in range(blocks):
        for row in range(4):
            target = group * blocks + i
            here = jnp.logical_and(target == g, r == row)
            index = i * 4 + row
            remote = pltpu.make_async_remote_copy(
                part.at[i], red.at[slot], red_send.at[index], red_recv.at[slot],
                device_id=(row, target), device_id_type=MESH)
            local = pltpu.make_async_copy(part.at[i], red.at[slot], red_recv.at[slot])
            transfers.append((here, remote))
            pl.when(here)(local.start)
            pl.when(jnp.logical_not(here))(remote.start)
    for s in range(grid):
        pltpu.make_async_copy(part.at[0], red.at[s], red_recv.at[s]).wait()
    squares = red[0]
    for s in range(1, grid):
        squares = squares + red[s]
    out_ref[...] = 1.0 / (squares / noise + LOADING)

    for here, remote in transfers:
        pl.when(jnp.logical_not(here))(remote.wait_send)
    for copy in pos_copies + row_copies + core_copies:
        copy.wait_send()
    others = ang.at[pl.ds(0, grid - 1)]
    pltpu.make_async_copy(others, others, ang_send).wait()


def body(rows, grid, positions, angles, subspace):
    parts, elements, columns = subspace.shape
    width = LANES * pl.cdiv(pl.cdiv(columns, 2), LANES)
    padded = jnp.pad(subspace, ((0, 0), (0, 0), (0, 2 * width - columns)))
    halves = jnp.moveaxis(padded.reshape(parts, elements, 2, width), 2, 0)
    per_block = angles.shape[1]
    blocks = grid // 4
    group_angles = blocks * per_block
    tiles = group_angles // TILE
    noise = columns * grid
    dma = pltpu.SemaphoreType.DMA
    out = pl.pallas_call(
        functools.partial(kernel, rows, grid, noise),
        out_shape=jax.ShapeDtypeStruct((1, per_block), jnp.float32),
        in_specs=[
            pl.BlockSpec(memory_space=pltpu.VMEM),
            pl.BlockSpec(memory_space=pltpu.VMEM),
            pl.BlockSpec(memory_space=pl.ANY),
        ],
        out_specs=pl.BlockSpec(memory_space=pltpu.VMEM),
        scratch_shapes=[
            pltpu.VMEM((4, 2, elements), jnp.int32),
            pltpu.VMEM((grid, 2, per_block), jnp.int32),
            pltpu.VMEM((2, group_angles, LANES), jnp.float32),
            pltpu.VMEM((4, 2, 2, elements, width), jnp.bfloat16),
            pltpu.VMEM((2 * TILE, 2 * elements), jnp.bfloat16),
            pltpu.VMEM((2 * TILE, 2 * elements), jnp.bfloat16),
            pltpu.VMEM((tiles, 2 * TILE, 2 * width), jnp.float32),
            pltpu.VMEM((blocks, 1, per_block), jnp.float32),
            pltpu.VMEM((grid, 1, per_block), jnp.float32),
            dma, dma, dma((4,)), dma((4,)), dma,
            dma((4,)), dma((4,)), dma((4,)), dma((4,)), dma((4 * blocks,)), dma((grid,)),
        ],
        compiler_params=pltpu.CompilerParams(collective_id=0, has_side_effects=True),
    )(positions, angles, halves)
    return out.reshape(per_block)


def solution(mesh):
    rows, grid = mesh.shape["rows"], mesh.shape["grid"]
    in_specs = (P(None, "rows"), P(None, "grid"), P(None, "rows", "grid"))
    fn = functools.partial(body, rows, grid)
    return jax.shard_map(fn, mesh=mesh, in_specs=in_specs, out_specs=P("grid"), check_vma=False)
```

```python
import functools

import jax
import jax.numpy as jnp
from jax import lax
from jax.experimental import pallas as pl
from jax.experimental.pallas import tpu as pltpu
from jax.sharding import PartitionSpec as P

PHASES = 4096
LOADING = 1e-06
MESH = pl.DeviceIdType.MESH
LANES = 128
SUBLANES = 16
TILE = 256
CHUNK = 32
SPAN = 2

COS_ODD = (-6.283164024353027, 41.33714294433594, -81.34076690673828, 70.9933853149414)
SIN_EVEN = (
    0.9999999403953552,
    -19.739171981811523,
    64.9345932006836,
    -85.24032592773438,
    56.242347717285156,
)


def horner(coefficients, x):
    total = coefficients[-1] * x + coefficients[-2]
    for c in coefficients[-3::-1]:
        total = total * x + c
    return total


def cos_sin(turns):
    r = turns - jnp.round(turns)
    w = jnp.abs(r) - 0.25
    w2 = w * w
    cos = horner(COS_ODD, w2) * w
    sin = horner(SIN_EVEN, w2)
    return cos, jnp.where(r < 0.0, -sin, sin)


def flip(bit, by):
    return 1 - bit if by else bit


def kernel(
    grid, noise, pos_ref, ang_ref, v_ref, out_ref,
    pos, ang, pcol, v, steering, acc, part, red,
    ang_send, ang_recv, pos_send, pos_recv, own_sem,
    row_send, row_recv, core_send, core_recv, red_send, red_recv,
):
    r, g = lax.axis_index("rows"), lax.axis_index("grid")
    half, y = r % 2, r // 2
    core, chip = g % 2, g // 2
    blocks = grid // 4
    group = y * 2 + core
    per_block = ang_ref.shape[1]
    elements = pos_ref.shape[1]
    width = v.shape[3]
    stored = v_ref.shape[1]
    shared = 2 * width - stored
    angles = steering.shape[2] // 2

    def row_partner(j):
        return flip(y, j // 2) * 2 + flip(half, j % 2)

    barrier = pltpu.get_barrier_semaphore()
    for j in range(1, 4):
        pl.semaphore_signal(barrier, inc=1, device_id=(row_partner(j), g), device_id_type=MESH)

    def greet(d, carry):
        pl.semaphore_signal(barrier, inc=1, device_id=(r, (g + d) % grid), device_id_type=MESH)
        return carry

    lax.fori_loop(1, grid, greet, 0)
    pl.semaphore_wait(barrier, 3 + grid - 1)

    pos_copies = []
    for j in range(1, 4):
        pos_copies.append(pltpu.make_async_remote_copy(
            pos_ref, pos.at[j], pos_send.at[j], pos_recv.at[j],
            device_id=(row_partner(j), g), device_id_type=MESH))
        pos_copies[-1].start()

    def send_angles(d, carry):
        pltpu.make_async_remote_copy(
            ang_ref, ang.at[g], ang_send, ang_recv,
            device_id=(r, (g + d) % grid), device_id_type=MESH).start()
        return carry

    lax.fori_loop(1, grid, send_angles, 0)
    pltpu.make_async_copy(ang_ref, ang.at[g], ang_recv).start()

    def share(which):
        return v_ref.at[:, pl.ds(pl.multiple_of(which * (stored - width), SUBLANES), width), :]

    row_copies = []
    for j in range(1, 4):
        row_copies.append(pltpu.make_async_remote_copy(
            share(flip(half, j % 2)), v.at[j, core], row_send.at[j], row_recv.at[j],
            device_id=(row_partner(j), g), device_id_type=MESH))

    def core_copy(j, source):
        return pltpu.make_async_remote_copy(
            source, v.at[j, core], core_send.at[j], core_recv.at[j],
            device_id=(r, chip * 2 + 1 - core), device_id_type=MESH)

    core_copies = [core_copy(0, share(half))] + [core_copy(j, v.at[j, core]) for j in range(1, 4)]
    row_copies[0].start()
    row_copies[1].start()
    core_copies[0].start()
    own_copy = pltpu.make_async_copy(share(half), v.at[0, core], own_sem)
    own_copy.start()

    def spread_positions(j):
        for k in range(2):
            line = (pos_ref[k : k + 1, :] if j == 0 else pos[j, k : k + 1, :]).astype(jnp.float32)
            pcol[k, j * elements : (j + 1) * elements, :] = jnp.broadcast_to(line, (LANES, elements)).T

    spread_positions(0)
    for j in range(1, 4):
        pos_copies[j - 1].wait_recv()
        spread_positions(j)
    row_copies[2].start()
    pltpu.make_async_copy(ang, ang, ang_recv).wait()

    def steer(j, first):
        @pl.loop(0, elements // CHUNK)
        def _(i):
            row = pl.multiple_of(i * CHUNK, CHUNK)
            p0 = pcol[0, pl.ds(j * elements + row, CHUNK), :]
            p1 = pcol[1, pl.ds(j * elements + row, CHUNK), :]
            for lane in range(0, angles, LANES):
                block = group * blocks + first + lane // per_block
                inner = lane % per_block
                a = ang[block, :, inner : inner + LANES].astype(jnp.float32) * (1.0 / PHASES)
                cos, sin = cos_sin(p0 * a[0:1] + p1 * a[1:2])
                steering[j, pl.ds(row, CHUNK), lane : lane + LANES] = cos.astype(jnp.bfloat16)
                steering[j, pl.ds(row, CHUNK), angles + lane : angles + lane + LANES] = sin.astype(jnp.bfloat16)

    def project(j):
        left = v[j].reshape(4 * width, elements)
        for tile in range(0, 2 * angles, TILE):
            product = jnp.dot(left, steering[j, :, tile : tile + TILE], preferred_element_type=jnp.float32)
            if j == 0:
                acc[:, :, tile : tile + TILE] = product.reshape(2, 2 * width, TILE)
            else:
                acc[:, :, tile : tile + TILE] += product.reshape(2, 2 * width, TILE)

    counted = lax.broadcasted_iota(jnp.int32, (width, TILE), 0) >= shared * half

    def finish(which, first, add):
        left = v[3, which].reshape(2 * width, elements)
        for tile in range(0, angles, TILE):
            with_cos = acc[which, :, tile : tile + TILE] + jnp.dot(
                left, steering[3, :, tile : tile + TILE], preferred_element_type=jnp.float32)
            with_sin = acc[which, :, angles + tile : angles + tile + TILE] + jnp.dot(
                left, steering[3, :, angles + tile : angles + tile + TILE], preferred_element_type=jnp.float32)
            real = with_cos[:width] + with_sin[width:]
            imag = with_sin[:width] - with_cos[width:]
            power = jnp.where(counted, real * real + imag * imag, 0.0)
            total = jnp.sum(power, axis=0, keepdims=True)
            block, inner = first + tile // per_block, tile % per_block
            if add:
                total = total + part[block, :, inner : inner + TILE]
            part[block, :, inner : inner + TILE] = total

    for first in range(0, blocks, angles // per_block):
        opening = first == 0
        steer(0, first)
        steer(1, first)
        if opening:
            for j in (1, 2):
                row_copies[j - 1].wait_recv()
                core_copies[j].start()
            own_copy.wait()
            core_copies[0].wait_recv()
        project(0)
        steer(2, first)
        steer(3, first)
        for j in (1, 2):
            if opening:
                core_copies[j].wait_recv()
            project(j)
        if opening:
            row_copies[2].wait_recv()
            core_copies[3].start()
        finish(core, first, False)
        if opening:
            core_copies[3].wait_recv()
        finish(1 - core, first, True)

    slot = half * (grid // 2) + chip
    transfers = []
    for i in range(blocks):
        for row in range(4):
            target = group * blocks + i
            here = jnp.logical_and(target == g, r == row)
            index = i * 4 + row
            remote = pltpu.make_async_remote_copy(
                part.at[i], red.at[slot], red_send.at[index], red_recv.at[slot],
                device_id=(row, target), device_id_type=MESH)
            local = pltpu.make_async_copy(part.at[i], red.at[slot], red_recv.at[slot])
            transfers.append((here, remote))
            pl.when(here)(local.start)
            pl.when(jnp.logical_not(here))(remote.start)
    for s in range(grid):
        pltpu.make_async_copy(part.at[0], red.at[s], red_recv.at[s]).wait()
    squares = red[0]
    for s in range(1, grid):
        squares = squares + red[s]
    out_ref[...] = 1.0 / (squares / noise + LOADING)

    for here, remote in transfers:
        pl.when(jnp.logical_not(here))(remote.wait_send)
    for copy in pos_copies + row_copies + core_copies:
        copy.wait_send()
    others = ang.at[pl.ds(0, grid - 1)]
    pltpu.make_async_copy(others, others, ang_send).wait()


def body(grid, positions, angles, subspace):
    parts, elements, columns = subspace.shape
    stored = SUBLANES * pl.cdiv(columns, SUBLANES)
    width = SUBLANES * pl.cdiv(stored, 2 * SUBLANES)
    by_column = jnp.swapaxes(subspace, 1, 2)
    if stored > columns:
        by_column = jnp.pad(by_column, ((0, 0), (0, stored - columns), (0, 0)))
    per_block = angles.shape[1]
    blocks = grid // 4
    span = min(SPAN, blocks) * per_block
    noise = columns * grid
    dma = pltpu.SemaphoreType.DMA
    out = pl.pallas_call(
        functools.partial(kernel, grid, noise),
        out_shape=jax.ShapeDtypeStruct((1, per_block), jnp.float32),
        in_specs=[
            pl.BlockSpec(memory_space=pltpu.VMEM),
            pl.BlockSpec(memory_space=pltpu.VMEM),
            pl.BlockSpec(memory_space=pl.ANY),
        ],
        out_specs=pl.BlockSpec(memory_space=pltpu.VMEM),
        scratch_shapes=[
            pltpu.VMEM((4, 2, elements), jnp.int32),
            pltpu.VMEM((grid, 2, per_block), jnp.int32),
            pltpu.VMEM((2, 4 * elements, LANES), jnp.float32),
            pltpu.VMEM((4, 2, 2, width, elements), jnp.bfloat16),
            pltpu.VMEM((4, elements, 2 * span), jnp.bfloat16),
            pltpu.VMEM((2, 2 * width, 2 * span), jnp.float32),
            pltpu.VMEM((blocks, 1, per_block), jnp.float32),
            pltpu.VMEM((grid, 1, per_block), jnp.float32),
            dma, dma, dma((4,)), dma((4,)), dma,
            dma((4,)), dma((4,)), dma((4,)), dma((4,)), dma((4 * blocks,)), dma((grid,)),
        ],
        compiler_params=pltpu.CompilerParams(collective_id=0, has_side_effects=True),
    )(positions, angles, by_column)
    return out.reshape(per_block)


def solution(mesh):
    in_specs = (P(None, "rows"), P(None, "grid"), P(None, "rows", "grid"))
    fn = functools.partial(body, mesh.shape["grid"])
    return jax.shard_map(fn, mesh=mesh, in_specs=in_specs, out_specs=P("grid"), check_vma=False)
```

```python
import functools

import jax
import jax.numpy as jnp
from jax import lax
from jax.experimental import pallas as pl
from jax.experimental.pallas import tpu as pltpu
from jax.sharding import PartitionSpec as P

PHASES = 4096
LOADING = 1e-06
MESH = pl.DeviceIdType.MESH
LANES = 128
SUBLANES = 16
TILE = 256
CHUNK = 64
SPAN = 2

COS_ODD = (-6.283164024353027, 41.33714294433594, -81.34076690673828, 70.9933853149414)
SIN_EVEN = (
    0.9999999403953552,
    -19.739171981811523,
    64.9345932006836,
    -85.24032592773438,
    56.242347717285156,
)


def horner(coefficients, x):
    total = coefficients[-1] * x + coefficients[-2]
    for c in coefficients[-3::-1]:
        total = total * x + c
    return total


def cos_sin(turns):
    r = turns - jnp.round(turns)
    w = jnp.abs(r) - 0.25
    w2 = w * w
    cos = horner(COS_ODD, w2) * w
    sin = horner(SIN_EVEN, w2)
    return cos, jnp.where(r < 0.0, -sin, sin)


def flip(bit, by):
    return 1 - bit if by else bit


def kernel(
    grid, noise, pos_ref, ang_ref, v_ref, out_ref,
    pos, ang, pcol, v, steering0, steering1, steering2, steering3, acc, part, red,
    ang_send, ang_recv, pos_send, pos_recv, own_sem,
    row_send, row_recv, core_send, core_recv, red_send, red_recv,
):
    steering = (steering0, steering1, steering2, steering3)
    r, g = lax.axis_index("rows"), lax.axis_index("grid")
    half, y = r % 2, r // 2
    core, chip = g % 2, g // 2
    blocks = grid // 4
    group = y * 2 + core
    per_block = ang_ref.shape[1]
    elements = pos_ref.shape[1]
    width = v.shape[3]
    stored = v_ref.shape[1]
    shared = 2 * width - stored
    angles = steering[0].shape[1] // 2

    def row_partner(j):
        return flip(y, j // 2) * 2 + flip(half, j % 2)

    barrier = pltpu.get_barrier_semaphore()
    for j in range(1, 4):
        pl.semaphore_signal(barrier, inc=1, device_id=(row_partner(j), g), device_id_type=MESH)

    def greet(d, carry):
        pl.semaphore_signal(barrier, inc=1, device_id=(r, (g + d) % grid), device_id_type=MESH)
        return carry

    lax.fori_loop(1, grid, greet, 0)
    pl.semaphore_wait(barrier, 3 + grid - 1)

    pos_copies = []
    for j in range(1, 4):
        pos_copies.append(pltpu.make_async_remote_copy(
            pos_ref, pos.at[j], pos_send.at[j], pos_recv.at[j],
            device_id=(row_partner(j), g), device_id_type=MESH))
        pos_copies[-1].start()

    def send_angles(d, carry):
        pltpu.make_async_remote_copy(
            ang_ref, ang.at[g], ang_send, ang_recv,
            device_id=(r, (g + d) % grid), device_id_type=MESH).start()
        return carry

    lax.fori_loop(1, grid, send_angles, 0)
    pltpu.make_async_copy(ang_ref, ang.at[g], ang_recv).start()

    def share(which):
        return v_ref.at[:, pl.ds(pl.multiple_of(which * (stored - width), SUBLANES), width), :]

    row_copies = []
    for j in range(1, 4):
        row_copies.append(pltpu.make_async_remote_copy(
            share(flip(half, j % 2)), v.at[j, core], row_send.at[j], row_recv.at[j],
            device_id=(row_partner(j), g), device_id_type=MESH))

    def core_copy(j, source):
        return pltpu.make_async_remote_copy(
            source, v.at[j, core], core_send.at[j], core_recv.at[j],
            device_id=(r, chip * 2 + 1 - core), device_id_type=MESH)

    core_copies = [core_copy(0, share(half))] + [core_copy(j, v.at[j, core]) for j in range(1, 4)]
    row_copies[0].start()
    row_copies[1].start()
    core_copies[0].start()
    own_copy = pltpu.make_async_copy(share(half), v.at[0, core], own_sem)
    own_copy.start()

    def spread_positions(j):
        for k in range(2):
            line = (pos_ref[k : k + 1, :] if j == 0 else pos[j, k : k + 1, :]).astype(jnp.float32)
            pcol[k, j * elements : (j + 1) * elements, :] = jnp.broadcast_to(line, (LANES, elements)).T

    spread_positions(0)
    for j in range(1, 4):
        pos_copies[j - 1].wait_recv()
        spread_positions(j)
    row_copies[2].start()
    pltpu.make_async_copy(ang, ang, ang_recv).wait()

    def steer_rows(j, first, row):
        p0 = pcol[0, pl.ds(j * elements + row, CHUNK), :]
        p1 = pcol[1, pl.ds(j * elements + row, CHUNK), :]
        for lane in range(0, angles, LANES):
            block = group * blocks + first + lane // per_block
            inner = lane % per_block
            a = ang[block, :, inner : inner + LANES].astype(jnp.float32) * (1.0 / PHASES)
            cos, sin = cos_sin(p0 * a[0:1] + p1 * a[1:2])
            steering[j][pl.ds(row, CHUNK), lane : lane + LANES] = cos.astype(jnp.bfloat16)
            steering[j][pl.ds(row, CHUNK), angles + lane : angles + lane + LANES] = sin.astype(jnp.bfloat16)

    def project_tile(j, start, size):
        left = v[j].reshape(4 * width, elements)
        columns = pl.ds(start, size)
        product = jnp.dot(left, steering[j][:, columns], preferred_element_type=jnp.float32)
        product = product.reshape(2, 2 * width, size)
        if j == 0:
            acc[:, :, columns] = product
        else:
            acc[:, :, columns] += product

    chunks = elements // CHUNK
    step = 2 * angles // chunks

    def sweep(j, first, begin, end):
        @pl.loop(begin, end)
        def _(i):
            if j > 0:
                project_tile(j - 1, pl.multiple_of(i * step, step), step)
            steer_rows(j, first, pl.multiple_of(i * CHUNK, CHUNK))

    counted = lax.broadcasted_iota(jnp.int32, (width, TILE), 0) >= shared * half

    def finish(which, first, add):
        left = v[3, which].reshape(2 * width, elements)
        for tile in range(0, angles, TILE):
            with_cos = acc[which, :, tile : tile + TILE] + jnp.dot(
                left, steering[3][:, tile : tile + TILE], preferred_element_type=jnp.float32)
            with_sin = acc[which, :, angles + tile : angles + tile + TILE] + jnp.dot(
                left, steering[3][:, angles + tile : angles + tile + TILE], preferred_element_type=jnp.float32)
            real = with_cos[:width] + with_sin[width:]
            imag = with_sin[:width] - with_cos[width:]
            power = jnp.where(counted, real * real + imag * imag, 0.0)
            total = jnp.sum(power, axis=0, keepdims=True)
            block, inner = first + tile // per_block, tile % per_block
            if add:
                total = total + part[block, :, inner : inner + TILE]
            part[block, :, inner : inner + TILE] = total

    for first in range(0, blocks, angles // per_block):
        opening = first == 0
        sweep(0, first, 0, chunks)
        if opening:
            own_copy.wait()
            core_copies[0].wait_recv()
        sweep(1, first, 0, 3 * chunks // 8)
        if opening:
            for j in (1, 2):
                row_copies[j - 1].wait_recv()
                core_copies[j].start()
        sweep(1, first, 3 * chunks // 8, chunks)
        if opening:
            core_copies[1].wait_recv()
        sweep(2, first, 0, chunks)
        if opening:
            core_copies[2].wait_recv()
        sweep(3, first, 0, chunks // 2)
        if opening:
            row_copies[2].wait_recv()
            core_copies[3].start()
        sweep(3, first, chunks // 2, chunks)
        finish(core, first, False)
        if opening:
            core_copies[3].wait_recv()
        finish(1 - core, first, True)

    slot = half * (grid // 2) + chip
    transfers = []
    for i in range(blocks):
        for row in range(4):
            target = group * blocks + i
            here = jnp.logical_and(target == g, r == row)
            index = i * 4 + row
            remote = pltpu.make_async_remote_copy(
                part.at[i], red.at[slot], red_send.at[index], red_recv.at[slot],
                device_id=(row, target), device_id_type=MESH)
            local = pltpu.make_async_copy(part.at[i], red.at[slot], red_recv.at[slot])
            transfers.append((here, remote))
            pl.when(here)(local.start)
            pl.when(jnp.logical_not(here))(remote.start)
    for s in range(grid):
        pltpu.make_async_copy(part.at[0], red.at[s], red_recv.at[s]).wait()
    squares = red[0]
    for s in range(1, grid):
        squares = squares + red[s]
    out_ref[...] = 1.0 / (squares / noise + LOADING)

    for here, remote in transfers:
        pl.when(jnp.logical_not(here))(remote.wait_send)
    for copy in pos_copies + row_copies + core_copies:
        copy.wait_send()
    others = ang.at[pl.ds(0, grid - 1)]
    pltpu.make_async_copy(others, others, ang_send).wait()


def body(grid, positions, angles, subspace):
    parts, elements, columns = subspace.shape
    stored = SUBLANES * pl.cdiv(columns, SUBLANES)
    width = SUBLANES * pl.cdiv(stored, 2 * SUBLANES)
    by_column = jnp.swapaxes(subspace, 1, 2)
    if stored > columns:
        by_column = jnp.pad(by_column, ((0, 0), (0, stored - columns), (0, 0)))
    per_block = angles.shape[1]
    blocks = grid // 4
    span = min(SPAN, blocks) * per_block
    noise = columns * grid
    dma = pltpu.SemaphoreType.DMA
    out = pl.pallas_call(
        functools.partial(kernel, grid, noise),
        out_shape=jax.ShapeDtypeStruct((1, per_block), jnp.float32),
        in_specs=[
            pl.BlockSpec(memory_space=pltpu.VMEM),
            pl.BlockSpec(memory_space=pltpu.VMEM),
            pl.BlockSpec(memory_space=pl.ANY),
        ],
        out_specs=pl.BlockSpec(memory_space=pltpu.VMEM),
        scratch_shapes=[
            pltpu.VMEM((4, 2, elements), jnp.int32),
            pltpu.VMEM((grid, 2, per_block), jnp.int32),
            pltpu.VMEM((2, 4 * elements, LANES), jnp.float32),
            pltpu.VMEM((4, 2, 2, width, elements), jnp.bfloat16),
            *[pltpu.VMEM((elements, 2 * span), jnp.bfloat16)] * 4,
            pltpu.VMEM((2, 2 * width, 2 * span), jnp.float32),
            pltpu.VMEM((blocks, 1, per_block), jnp.float32),
            pltpu.VMEM((grid, 1, per_block), jnp.float32),
            dma, dma, dma((4,)), dma((4,)), dma,
            dma((4,)), dma((4,)), dma((4,)), dma((4,)), dma((4 * blocks,)), dma((grid,)),
        ],
        compiler_params=pltpu.CompilerParams(collective_id=0, has_side_effects=True),
    )(positions, angles, by_column)
    return out.reshape(per_block)


def solution(mesh):
    in_specs = (P(None, "rows"), P(None, "grid"), P(None, "rows", "grid"))
    fn = functools.partial(body, mesh.shape["grid"])
    return jax.shard_map(fn, mesh=mesh, in_specs=in_specs, out_specs=P("grid"), check_vma=False)
```
